32 devices in a mesh: ep: 8 (over z, y), zr: 4 (over x, core).
Axes of the slice: x: 2, y: 2, z: 4, core: 2. Of those that a mesh axis runs over, the one named last changes fastest.
Arguments:
- tokens: bfloat16 [4096, 1024], P(('ep', 'zr')), may hold values from -6 to 6
- cotangent: bfloat16 [4096, 1024], P(('ep', 'zr')), may hold values from -6 to 6
- gates: bfloat16 [4096, 2], P(('ep', 'zr')), may hold values from 0.099609375 to 0.8984375
- experts: int32 [4096, 2], P(('ep', 'zr')), may hold values from 0 to 7, all different within a row; in each aligned block of 128 rows (0 to 127, 128 to 255, ...) at most 48 rows name the same one
- keep: int32 [4096, 2], P(('ep', 'zr')), may hold values 0 or 1
- gate_w: bfloat16 [8, 1024, 1024], P('ep', None, 'zr'), may hold values from -0.1875 to 0.1875
- up_w: bfloat16 [8, 1024, 1024], P('ep', None, 'zr'), may hold values from -0.1875 to 0.1875
- down_w: bfloat16 [8, 1024, 1024], P('ep', 'zr'), may hold values from -0.1875 to 0.1875
Outputs:
- d_tokens: bfloat16 [4096, 1024], P(('ep', 'zr'))
- d_gates: bfloat16 [4096, 2], P(('ep', 'zr'))
- d_gate_w: bfloat16 [8, 1024, 1024], P('ep', None, 'zr')
- d_up_w: bfloat16 [8, 1024, 1024], P('ep', None, 'zr')
- d_down_w: bfloat16 [8, 1024, 1024], P('ep', 'zr')
The draws below stay inside these ranges and needn't reach their ends.
Inputs may be any that keep to these rules, and one draw needn't show every extreme that they name: Each row names two different experts. Among the 128 rows of one device no expert is named more than 48 times, and in every draw some expert is named exactly 48 times by the rows of some device.
All inputs are finite; a program needn't handle non-finite values. No bound on the sum of `keep` on one device may be relied on, other than what follows from the above.
Results may differ from the reference program's by a relative error of at most 0.012.
Values may be sent and summed in bfloat16 or wider, within the bound.
No kernel may reach another device: no remote copies, remote signals or barrier semaphores. Data moves between devices by JAX's collectives and lax.ppermute only.
A program may use at most 64 MiB of HBM per device.

```python
import math
import jax
import jax.numpy as jnp
import numpy as np
from jax import lax

D = 1024
H = 1024
HIDDEN_QUARTER = 256
TOK_DEV = 128
EXPERTS = 8
CAP = 48
TOKENS = 4096
N_EP = 8
N_ZR = 4


def place_ends(result, stream_key, low, high):
    place = [jax.random.randint(jax.random.fold_in(stream_key, axis), (), 0, length) for axis, length in enumerate(result.shape)]
    longest = result.shape.index(max(result.shape))
    next_to = place[:longest] + [(place[longest] + 1) % result.shape[longest]] + place[longest + 1:]
    return result.at[tuple(place)].set(low).at[tuple(next_to)].set(high)


def block_levels(stream_key, shape, split, smallest, top_value):
    gain, own = 1.0, jax.random.fold_in(stream_key, 6)
    for dim, shards_of in split:
        draws = jnp.exp(jax.random.uniform(jax.random.fold_in(own, dim), (shards_of,), jnp.float32, smallest / len(split), top_value / len(split)))
        gain = gain * jnp.repeat(draws, shape[dim] // shards_of).reshape([-1 if axis == dim else 1 for axis in range(len(shape))])
    return gain


def shared_out(stream_key, own, number, rows, amount, top, reach, lean):
    sequence = jax.random.permutation(stream_key, amount)
    packed, ordinary = portions_of(amount, rows * top, reach, lean, True), portions_of(amount, rows * top, reach, lean, False)
    places = jnp.arange(amount)

    def named(lengths, rotation):
        used = int((lengths > 0).sum())
        fixed = max(1, used // 4)
        shifted = fixed + (places - fixed + rotation * (used - fixed)) % max(1, amount - fixed)
        return jnp.zeros((amount,), jnp.int32).at[sequence[jnp.where(places < fixed, places, shifted)]].set(jnp.asarray(lengths, jnp.int32))

    lengths = jnp.where(number % 4 == 0, named(packed, number // 4), named(ordinary, number - number // 4 - 1))
    mixed = jax.random.permutation(jax.random.fold_in(own, 3), amount)
    donor, taker = mixed[0:amount // 2 * 2:2], mixed[1:amount // 2 * 2:2]
    margin = jnp.minimum(lengths[donor] - 1, reach - lengths[taker]) // 2
    margin = jnp.where((donor == sequence[0]) | (taker == sequence[0]) | (lengths[taker] == 0), 0, jnp.maximum(margin, 0))
    shifted = jax.random.randint(jax.random.fold_in(own, 4), (amount // 2,), 0, 1 << 20) % (margin + 1)
    lengths = lengths.at[donor].add(-shifted).at[taker].add(shifted)
    members = jnp.searchsorted(jnp.cumsum(lengths), jnp.arange(rows * top), side="right").astype(jnp.int32)
    listing = members.reshape(top, rows).T
    listing = listing[jax.random.permutation(jax.random.fold_in(own, 1), rows)]
    rotation = jax.random.randint(jax.random.fold_in(own, 2), (rows, 1), 0, top)
    return jnp.take_along_axis(listing, (jnp.arange(top)[None, :] + rotation) % top, axis=1)


def portions_of(amount, total, bound, lean, full):
    portions = [(1 << 20) // math.isqrt(grade ** lean) + 1 for grade in range(1, amount + 1)]
    largest = bound if full else min(bound, max(-(-total // amount), total * portions[0] // sum(portions)))
    least = 1 if total - largest >= amount - 1 else 0
    given, spare = [largest] + [least] * (amount - 1), total - largest - least * (amount - 1)
    while spare > 0:
        candidates = [i for i in range(1, amount) if given[i] < largest] or [i for i in range(1, amount) if given[i] < bound]
        mass, left = sum([portions[i] for i in candidates]), spare
        for i in candidates:
            more = min(bound - given[i], max(1, left * portions[i] // mass), spare)
            given[i] = given[i] + more
            spare = spare - more
    return np.array(given)


def gaussian(key, shape, width, limit, pieces=(), kind=jnp.bfloat16):
    values = width * jax.random.normal(key, shape, jnp.float32)
    if pieces:
        values = values * block_levels(key, shape, pieces, -0.22, 0.18)
    return jnp.clip(values, -limit, limit).astype(kind)


def setup_inputs(seed: int = 0) -> dict:
    seeds = jax.random.split(jax.random.key(seed), 9)
    tokens = gaussian(seeds[0], (TOKENS, D), 1.0, 6.0, ((0, 32),))
    cotangent = gaussian(seeds[1], (TOKENS, D), 1.0, 6.0, ((0, 32),))
    gates = jnp.clip(0.099609375 + 0.7988281 * jax.random.uniform(seeds[2], (TOKENS, 2), jnp.float32) ** block_levels(seeds[2], (TOKENS, 2), ((0, 32),), -0.2, 0.2), 0.099609375, 0.8984375).astype(jnp.bfloat16)
    experts_keys = jax.random.split(jax.random.fold_in(seeds[3], 1), TOKENS // TOK_DEV)
    experts_turns = jax.random.permutation(jax.random.fold_in(seeds[3], 3), TOKENS // TOK_DEV)
    experts = jax.vmap(lambda own, number: shared_out(jax.random.fold_in(seeds[3], 2), own, number, TOK_DEV, EXPERTS, 2, CAP, 2))(experts_keys, experts_turns).reshape((TOKENS, 2))
    keep = place_ends((jax.random.randint(seeds[4], (TOKENS, 2), 0, 8) < 7).astype(jnp.int32), jax.random.fold_in(seeds[4], 1), 0, 1)
    gate_w = gaussian(seeds[5], (EXPERTS, D, H), D ** -0.5, 0.1875, ((0, 8), (2, 4)))
    up_w = gaussian(seeds[6], (EXPERTS, D, H), D ** -0.5, 0.1875, ((0, 8), (2, 4)))
    down_w = gaussian(seeds[7], (EXPERTS, H, D), H ** -0.5, 0.1875, ((0, 8), (1, 4)))
    return {"tokens": tokens, "cotangent": cotangent, "gates": gates, "experts": experts, "keep": keep, "gate_w": gate_w, "up_w": up_w, "down_w": down_w}


def reference(tokens, cotangent, gates, experts, keep, gate_w, up_w, down_w):
    ndevices = N_EP * N_ZR
    assigned = TOK_DEV * 2
    flat_exp = experts.reshape(ndevices, assigned)
    onehot = (flat_exp[:, :, None] == jnp.arange(EXPERTS, dtype=jnp.int32)[None, None, :]).astype(jnp.int32)
    before = jnp.cumsum(onehot, axis=1) - onehot
    position = jnp.sum(before * onehot, axis=2)
    dest = flat_exp * CAP + position
    dev_index = jnp.broadcast_to(jnp.arange(ndevices, dtype=jnp.int32)[:, None], (ndevices, assigned))
    global_ids = dev_index * assigned + jnp.arange(assigned, dtype=jnp.int32)[None, :]
    slot_owner = jnp.full((ndevices, EXPERTS * CAP), -1, jnp.int32).at[dev_index, dest].set(global_ids)
    weight_flat = gates.reshape(-1).astype(jnp.float32) * keep.reshape(-1).astype(jnp.float32)

    def per_expert(expert):
        owners = lax.dynamic_slice(slot_owner, (jnp.int32(0), (expert * CAP).astype(jnp.int32)), (ndevices, CAP)).reshape(-1)
        valid = owners >= 0
        safe = jnp.where(valid, owners, 0)
        tok_index = safe // 2
        slot_input_rows = jnp.where(valid[:, None], tokens[tok_index], jnp.zeros((), jnp.bfloat16))
        slot_g = jnp.where(valid[:, None], cotangent[tok_index], jnp.zeros((), jnp.bfloat16))
        slot_w = jnp.where(valid, weight_flat[safe], jnp.float32(0.0))
        wg = gate_w[expert]
        wu = up_w[expert]
        wd = down_w[expert]
        pre_a = jnp.dot(slot_input_rows, wg, preferred_element_type=jnp.float32)
        pre_b = jnp.dot(slot_input_rows, wu, preferred_element_type=jnp.float32)
        sig = 1.0 / (1.0 + jnp.exp(-pre_a))
        act = pre_a * sig
        hidden_activation = act * pre_b
        value_gradient = jnp.dot(slot_g, wd.T, preferred_element_type=jnp.float32)
        dh = slot_w[:, None] * value_gradient
        gate_branch_gradient = (dh * pre_b * sig * (1.0 + pre_a * (1.0 - sig))).astype(jnp.bfloat16)
        up_branch_gradient = (dh * act).astype(jnp.bfloat16)
        hidden_w = (slot_w[:, None] * hidden_activation).astype(jnp.bfloat16)
        dwg = jnp.dot(slot_input_rows.T, gate_branch_gradient, preferred_element_type=jnp.float32).astype(jnp.bfloat16)
        dwu = jnp.dot(slot_input_rows.T, up_branch_gradient, preferred_element_type=jnp.float32).astype(jnp.bfloat16)
        dwd = jnp.dot(hidden_w.T, slot_g, preferred_element_type=jnp.float32).astype(jnp.bfloat16)
        slot_count = slot_input_rows.shape[0]
        gate_quarter_slice = gate_branch_gradient.astype(jnp.float32).reshape(slot_count, N_ZR, HIDDEN_QUARTER)
        up_quarter_slice = up_branch_gradient.astype(jnp.float32).reshape(slot_count, N_ZR, HIDDEN_QUARTER)
        wg_q = wg.astype(jnp.float32).reshape(D, N_ZR, HIDDEN_QUARTER)
        wu_q = wu.astype(jnp.float32).reshape(D, N_ZR, HIDDEN_QUARTER)
        part_x = jnp.einsum("szh,dzh->szd", gate_quarter_slice, wg_q) + jnp.einsum("szh,dzh->szd", up_quarter_slice, wu_q)
        part_x = lax.optimization_barrier(part_x.astype(jnp.bfloat16))
        slot_dx = jnp.sum(part_x.astype(jnp.float32), axis=1).astype(jnp.bfloat16)
        partial_gate_rows = jnp.sum((hidden_activation * value_gradient).reshape(slot_count, N_ZR, HIDDEN_QUARTER), axis=2)
        partial_gate_rows = lax.optimization_barrier(partial_gate_rows.astype(jnp.bfloat16))
        slot_dg = jnp.sum(partial_gate_rows.astype(jnp.float32), axis=1).astype(jnp.bfloat16)
        marked = jnp.where(valid, owners, jnp.int32(TOKENS * 2))
        return dwg, dwu, dwd, slot_dx, slot_dg, marked

    dwg, dwu, dwd, slot_dx, slot_dg, marked = lax.map(per_expert, jnp.arange(EXPERTS, dtype=jnp.int32))
    marked = marked.reshape(-1)
    slot_dx = slot_dx.reshape(-1, D)
    slot_dg = slot_dg.reshape(-1)
    tok_target = jnp.where(marked < TOKENS * 2, marked // 2, jnp.int32(TOKENS))
    d_tokens = jnp.zeros((TOKENS, D), jnp.float32).at[tok_target].add(slot_dx.astype(jnp.float32), mode="drop")
    gate_flat = jnp.zeros((TOKENS * 2,), jnp.bfloat16).at[marked].set(slot_dg, mode="drop")
    d_gates = (gate_flat * keep.reshape(-1).astype(jnp.bfloat16)).reshape(TOKENS, 2)
    return d_tokens.astype(jnp.bfloat16), d_gates, dwg, dwu, dwd
```

```python
import functools

import jax
import jax.numpy as jnp
from jax import lax
from jax.experimental import pallas as pl
from jax.experimental.pallas import tpu as pltpu
from jax.sharding import PartitionSpec as P


F32 = jnp.float32
BF16 = jnp.bfloat16
LANES = 128


def contract(a, b, dim_a, dim_b):
    return lax.dot_general(a, b, (((dim_a,), (dim_b,)), ((), ())), preferred_element_type=F32)


def send_kernel(n_experts, capacity, me_ref, exp_ref, keep_ref, gate_ref, tok_ref, cot_ref, *outs):
    rows = tok_ref.shape[0]
    table_ref, messages = outs[0], outs[1:]
    me = me_ref[0]
    t_in = lax.broadcasted_iota(jnp.int32, (rows, rows), 0)
    t_out = lax.broadcasted_iota(jnp.int32, (rows, rows), 1)
    eye = (t_in == t_out).astype(BF16)
    earlier = (t_in < t_out).astype(BF16)
    weight = gate_ref[...].astype(F32) * keep_ref[...].astype(F32)
    exp_t = contract(exp_ref[...].astype(F32).astype(BF16), eye, 0, 0)
    weight_t = contract(weight.astype(BF16), eye, 0, 0)
    ids = lax.broadcasted_iota(jnp.int32, (n_experts, rows), 0) ^ me
    ids = ids.astype(F32)
    named0 = exp_t[0:1, :] == ids
    named1 = exp_t[1:2, :] == ids
    named = named0 | named1
    w_of = jnp.where(named0, weight_t[0:1, :], 0.0) + jnp.where(named1, weight_t[1:2, :], 0.0)
    position = contract(named.astype(F32).astype(BF16), earlier, 1, 0)
    position = jnp.where(named, position, -1.0)
    slots = lax.broadcasted_iota(jnp.int32, (capacity, rows), 0).astype(F32)
    for k in range(n_experts):
        hit = slots == position[k : k + 1, :]
        table = jnp.where(hit, 1.0, 0.0).astype(BF16)
        table_w = jnp.where(hit, w_of[k : k + 1, :], 0.0).astype(BF16)
        table_ref[k * capacity : (k + 1) * capacity, :] = table
        messages[k][0:capacity, :] = contract(table, tok_ref[...], 1, 0).astype(BF16)
        messages[k][capacity:, :] = contract(table_w, cot_ref[...], 1, 0).astype(BF16)


def grad_kernel(n_msgs, capacity, *refs):
    msgs = refs[:n_msgs]
    wg_refs, wu_refs, wd_refs = refs[n_msgs : n_msgs + 2], refs[n_msgs + 2 : n_msgs + 4], refs[n_msgs + 4 : n_msgs + 6]
    outs = refs[n_msgs + 6 :]
    back, (da_ref, db_ref, h_ref) = outs[:n_msgs], outs[n_msgs:]
    width = msgs[0].shape[1]
    x = jnp.concatenate([m[0:capacity, :] for m in msgs], axis=0)
    gw = jnp.concatenate([m[capacity:, :] for m in msgs], axis=0)
    part_x = None
    part_g = None
    for q in range(2):
        a = contract(x, wg_refs[q][...], 1, 0)
        b = contract(x, wu_refs[q][...], 1, 0)
        dh = contract(gw, wd_refs[q][...], 1, 1)
        sig = 1.0 / (1.0 + jnp.exp(-a))
        act = a * sig
        h = act * b
        da = (dh * b * sig * (1.0 + a * (1.0 - sig))).astype(BF16)
        db = (dh * act).astype(BF16)
        hidden = a.shape[1]
        cols = slice(q * hidden, (q + 1) * hidden)
        da_ref[:, cols] = da
        db_ref[:, cols] = db
        h_ref[:, cols] = h.astype(BF16)
        px = contract(da, wg_refs[q][...], 1, 1) + contract(db, wu_refs[q][...], 1, 1)
        pg = jnp.sum(h * dh, axis=1, keepdims=True)
        part_x = px if part_x is None else part_x + px
        part_g = pg if part_g is None else part_g + pg
    for m in range(n_msgs):
        rows = slice(m * capacity, (m + 1) * capacity)
        back[m][:, 0:width] = part_x[rows, :].astype(BF16)
        back[m][:, width:] = jnp.broadcast_to(part_g[rows, :], (capacity, LANES)).astype(BF16)


def weight_kernel(counts, capacity, quarter, has_received, *refs):
    n_msgs = sum(counts)
    msgs, refs = refs[:n_msgs], refs[n_msgs:]
    das, refs = refs[: len(counts)], refs[len(counts) :]
    dbs, refs = refs[: len(counts)], refs[len(counts) :]
    hs, refs = refs[: len(counts)], refs[len(counts) :]
    received, outs = (refs[:3], refs[3:]) if has_received else (None, refs)
    hidden = outs[2].shape[0]
    cols = slice(quarter * hidden, (quarter + 1) * hidden)
    x = jnp.concatenate([m[0:capacity, :] for m in msgs], axis=0)
    gw = jnp.concatenate([m[capacity:, :] for m in msgs], axis=0)
    da = jnp.concatenate([r[:, cols] for r in das], axis=0)
    db = jnp.concatenate([r[:, cols] for r in dbs], axis=0)
    h = jnp.concatenate([r[:, cols] for r in hs], axis=0)
    results = (contract(x, da, 0, 0), contract(x, db, 0, 0), contract(h, gw, 0, 0))
    for i in range(3):
        total = results[i]
        if has_received:
            total = total + received[i][...].astype(F32)
        outs[i][...] = total.astype(BF16)


def sum_kernel(n_msgs, n_parts, *refs):
    outs = refs[n_msgs * n_parts :]
    for m in range(n_msgs):
        total = refs[m * n_parts][...].astype(F32)
        for p in range(1, n_parts):
            total = total + refs[m * n_parts + p][...].astype(F32)
        outs[m][...] = total.astype(BF16)


def combine_kernel(n_experts, capacity, me_ref, exp_ref, keep_ref, gate_ref, table_ref, *refs):
    msgs, (dtok_ref, dgate_ref) = refs[:n_experts], refs[n_experts:]
    width = dtok_ref.shape[1]
    me = me_ref[0]
    rows = jnp.concatenate([m[:, 0:width] for m in msgs], axis=0)
    dtok_ref[...] = contract(table_ref[...], rows, 0, 0).astype(BF16)
    experts = exp_ref[...]
    d_gates = jnp.zeros(experts.shape, F32)
    for k in range(n_experts):
        value = contract(table_ref[k * capacity : (k + 1) * capacity, :], msgs[k][:, width:], 0, 0)
        d_gates = d_gates + jnp.where(experts == (me ^ k), value[:, 0 : experts.shape[1]], 0.0)
    d_gates = d_gates * keep_ref[...].astype(F32) / gate_ref[...].astype(F32)
    dgate_ref[...] = d_gates.astype(BF16)


def call(body, outs, n_in, smem=0, cost=None):
    vmem = pl.BlockSpec(memory_space=pltpu.VMEM)
    scalar = pl.BlockSpec(memory_space=pltpu.SMEM)
    return pl.pallas_call(
        body,
        out_shape=[jax.ShapeDtypeStruct(shape, BF16) for shape in outs],
        in_specs=[scalar] * smem + [vmem] * (n_in - smem),
        out_specs=[vmem] * len(outs),
        cost_estimate=cost,
        name=body.func.__name__,
    )


def local_tiled(tokens, cotangent, gates, experts, keep, gate_w, up_w, down_w):
    n_experts = lax.axis_size("ep")
    n_groups = lax.axis_size("zr")
    tok_rows, width = tokens.shape
    hidden = gate_w.shape[2]
    capacity = 3 * tok_rows // n_experts
    me = lax.axis_index("ep").astype(jnp.int32).reshape(1)

    def exchange(value, axis, size, bit):
        return lax.ppermute(value, axis, [(i, i ^ bit) for i in range(size)])

    weights = [(w[0], exchange(w[0], "zr", n_groups, 1)) for w in (gate_w, up_w, down_w)]
    weights = [w for pair in weights for w in pair]

    outs = [(n_experts * capacity, tok_rows)] + [(2 * capacity, width)] * n_experts
    table, *sends = call(functools.partial(send_kernel, n_experts, capacity), outs, 6, smem=1)(
        me, experts, keep, gates, tokens, cotangent
    )
    order = list(range(n_experts // 2, n_experts)) + list(range(n_experts // 2 - 1, -1, -1))
    mine = {k: exchange(sends[k], "ep", n_experts, k) if k else sends[0] for k in order}
    peers = list(range(2, n_groups, 2))
    theirs = {k: [exchange(mine[k], "zr", n_groups, r) for r in peers] for k in order}

    half = n_experts // 4
    groups = [list(range(n_experts // 2 + half)), list(range(n_experts // 2 + half, n_experts))]
    n_parts = 1 + len(peers)
    all_msgs, counts, das, dbs, hs, returned = [], [], [], [], [], {}
    for group in groups:
        msgs = [mine[k] for k in group] + [theirs[k][p] for p in range(len(peers)) for k in group]
        n_rows = len(msgs) * capacity
        outs = [(capacity, width + LANES)] * len(msgs) + [(n_rows, 2 * hidden)] * 3
        results = call(functools.partial(grad_kernel, len(msgs), capacity), outs, len(msgs) + 6)(*msgs, *weights)
        back = results[: len(msgs)]
        da, db, h = results[len(msgs) :]
        all_msgs, counts = all_msgs + msgs, counts + [len(msgs)]
        das, dbs, hs = das + [da], dbs + [db], hs + [h]
        parts = []
        for i, k in enumerate(group):
            parts.append(back[i])
            for p, r in enumerate(peers):
                parts.append(exchange(back[(p + 1) * len(group) + i], "zr", n_groups, r))
        summed = call(
            functools.partial(sum_kernel, len(group), n_parts), [(capacity, width + LANES)] * len(group), len(parts)
        )(*parts)
        for i, k in enumerate(group):
            returned[k] = exchange(summed[i], "ep", n_experts, k) if k else summed[i]

    w_outs = [(width, hidden), (width, hidden), (hidden, width)]
    w_args = all_msgs + das + dbs + hs
    partner = call(functools.partial(weight_kernel, counts, capacity, 1, False), w_outs, len(w_args))(*w_args)
    received = [exchange(w, "zr", n_groups, 1) for w in partner]
    w_args = w_args + received
    dwg, dwu, dwd = call(functools.partial(weight_kernel, counts, capacity, 0, True), w_outs, len(w_args))(*w_args)

    outs = [(tok_rows, width), experts.shape]
    d_tokens, d_gates = call(functools.partial(combine_kernel, n_experts, capacity), outs, 5 + n_experts, smem=1)(
        me, experts, keep, gates, table, *[returned[k] for k in range(n_experts)]
    )
    return d_tokens, d_gates, dwg[None], dwu[None], dwd[None]


def route_tables(experts, keep, gates, n_experts, capacity):
    tok_rows = experts.shape[0]
    flat_exp = experts.reshape(-1)
    onehot = (flat_exp[:, None] == jnp.arange(n_experts, dtype=jnp.int32)[None, :]).astype(
        jnp.int32
    )
    before = jnp.cumsum(onehot, axis=0) - onehot
    position = jnp.sum(before * onehot, axis=1)
    dest = (flat_exp * capacity + position).reshape(tok_rows, 2)
    slot_ids = jnp.arange(n_experts * capacity, dtype=jnp.int32)
    matches = dest[None, :, :] == slot_ids[:, None, None]
    table = jnp.any(matches, axis=2).astype(jnp.bfloat16)
    weight = gates.astype(jnp.float32) * keep.astype(jnp.float32)
    slot_weight = jnp.sum(jnp.where(matches, weight[None, :, :], 0.0), axis=(1, 2))
    return (table, dest, slot_weight)


def expert_grads(slot_input_rows, slot_g, slot_w, wg, wu, wd):
    pre_a = jnp.dot(slot_input_rows, wg, preferred_element_type=jnp.float32)
    pre_b = jnp.dot(slot_input_rows, wu, preferred_element_type=jnp.float32)
    sig = 1.0 / (1.0 + jnp.exp(-pre_a))
    act = pre_a * sig
    hidden_activation = act * pre_b
    value_gradient = jnp.einsum("sd,hd->sh", slot_g, wd, preferred_element_type=jnp.float32)
    scale = slot_w.astype(jnp.float32)[:, None]
    dh = scale * value_gradient
    gate_branch_gradient = (dh * pre_b * sig * (1.0 + pre_a * (1.0 - sig))).astype(jnp.bfloat16)
    up_branch_gradient = (dh * act).astype(jnp.bfloat16)
    hidden_w = (scale * hidden_activation).astype(jnp.bfloat16)
    dwg = jnp.einsum(
        "sd,sh->dh", slot_input_rows, gate_branch_gradient, preferred_element_type=jnp.float32
    ).astype(jnp.bfloat16)
    dwu = jnp.einsum(
        "sd,sh->dh", slot_input_rows, up_branch_gradient, preferred_element_type=jnp.float32
    ).astype(jnp.bfloat16)
    dwd = jnp.einsum("sh,sd->hd", hidden_w, slot_g, preferred_element_type=jnp.float32).astype(
        jnp.bfloat16
    )
    part_x = jnp.einsum("sh,dh->sd", gate_branch_gradient, wg, preferred_element_type=jnp.float32)
    part_x = part_x + jnp.einsum(
        "sh,dh->sd", up_branch_gradient, wu, preferred_element_type=jnp.float32
    )
    partial_gate_rows = jnp.sum(hidden_activation * value_gradient, axis=1)
    return (dwg, dwu, dwd, part_x.astype(jnp.bfloat16), partial_gate_rows.astype(jnp.bfloat16))


def local_general(tokens, cotangent, gates, experts, keep, gate_w, up_w, down_w):
    n_experts = lax.axis_size("ep")
    n_groups = lax.axis_size("zr")
    tok_rows = tokens.shape[0]
    width = tokens.shape[1]
    capacity = max(2, 3 * tok_rows // n_experts)
    flat_width = capacity * width
    table, dest, slot_weight = route_tables(experts, keep, gates, n_experts, capacity)
    send_x = jnp.dot(table, tokens, preferred_element_type=jnp.float32).astype(jnp.bfloat16)
    send_g = jnp.dot(table, cotangent, preferred_element_type=jnp.float32).astype(jnp.bfloat16)
    send_x = send_x.reshape(1, n_experts, flat_width)
    send_g = send_g.reshape(1, n_experts, flat_width)
    send_w = slot_weight.astype(jnp.bfloat16).reshape(1, n_experts, capacity)
    moved = (
        lax.all_to_all(send_x, "ep", split_axis=1, concat_axis=1, tiled=True),
        lax.all_to_all(send_g, "ep", split_axis=1, concat_axis=1, tiled=True),
        lax.all_to_all(send_w, "ep", split_axis=1, concat_axis=1, tiled=True),
    )
    arrived = (
        lax.all_gather(moved[0], "zr", axis=0, tiled=True),
        lax.all_gather(moved[1], "zr", axis=0, tiled=True),
        lax.all_gather(moved[2], "zr", axis=0, tiled=True),
    )
    slot_input_rows = arrived[0].reshape(-1, width)
    slot_g = arrived[1].reshape(-1, width)
    slot_w = arrived[2].reshape(-1)
    dwg, dwu, dwd, part_x, partial_gate_rows = expert_grads(
        slot_input_rows, slot_g, slot_w, gate_w[0], up_w[0], down_w[0]
    )
    part_x = part_x.reshape(n_groups, n_experts, flat_width)
    partial_gate_rows = partial_gate_rows.reshape(n_groups, n_experts, capacity)
    summed = (
        lax.psum_scatter(
            part_x.astype(jnp.float32).astype(jnp.bfloat16), "zr", scatter_dimension=0, tiled=True
        ).astype(jnp.float32),
        lax.psum_scatter(
            partial_gate_rows.astype(jnp.float32).astype(jnp.bfloat16),
            "zr",
            scatter_dimension=0,
            tiled=True,
        ).astype(jnp.float32),
    )
    rounded = (summed[0].astype(jnp.bfloat16), summed[1].astype(jnp.bfloat16))
    returned = (
        lax.all_to_all(rounded[0], "ep", split_axis=1, concat_axis=1, tiled=True),
        lax.all_to_all(rounded[1], "ep", split_axis=1, concat_axis=1, tiled=True),
    )
    slot_dx = returned[0]
    slot_dg = returned[1]
    slot_dx = slot_dx.reshape(n_experts * capacity, width)
    slot_dg = slot_dg.reshape(n_experts * capacity)
    d_tokens = jnp.einsum("st,sd->td", table, slot_dx, preferred_element_type=jnp.float32).astype(
        jnp.bfloat16
    )
    d_gates = jnp.take(slot_dg, dest) * keep.astype(jnp.bfloat16)
    return (d_tokens, d_gates, dwg[None], dwu[None], dwd[None])


def pick(mesh):
    def local(tokens, *rest):
        n_experts, n_groups = lax.axis_size("ep"), lax.axis_size("zr")
        capacity = 3 * tokens.shape[0] // n_experts
        paired = n_experts & (n_experts - 1) == 0 and n_groups & (n_groups - 1) == 0 and n_groups > 1
        tiled = capacity % 16 == 0 and tokens.shape[1] % LANES == 0
        return (local_tiled if paired and tiled else local_general)(tokens, *rest)

    return local


def solution(mesh):
    placed = (
        P(("ep", "zr"), None),
        P(("ep", "zr"), None),
        P(("ep", "zr"), None),
        P(("ep", "zr"), None),
        P(("ep", "zr"), None),
        P("ep", None, "zr"),
        P("ep", None, "zr"),
        P("ep", "zr", None),
    )
    return jax.shard_map(
        pick(mesh),
        mesh=mesh,
        in_specs=placed,
        out_specs=(
            P(("ep", "zr"), None),
            P(("ep", "zr"), None),
            P("ep", None, "zr"),
            P("ep", None, "zr"),
            P("ep", "zr", None),
        ),
        check_vma=False,
    )
```

```python
import functools

import jax
import jax.numpy as jnp
from jax import lax
from jax.experimental import pallas as pl
from jax.experimental.pallas import tpu as pltpu
from jax.sharding import PartitionSpec as P


F32 = jnp.float32
BF16 = jnp.bfloat16
LANES = 128
VMEM_LIMIT = 24 * 1024 * 1024


def contract(a, b, dim_a, dim_b):
    return lax.dot_general(a, b, (((dim_a,), (dim_b,)), ((), ())), preferred_element_type=F32)


def send_kernel(n_experts, capacity, me_ref, exp_ref, keep_ref, gate_ref, tok_ref, cot_ref, *outs):
    rows = tok_ref.shape[0]
    table_ref, messages = outs[0], outs[1:]
    earlier = lax.broadcasted_iota(jnp.int32, (rows, rows), 0) < lax.broadcasted_iota(jnp.int32, (rows, rows), 1)
    weight = gate_ref[...].astype(F32) * keep_ref[...].astype(F32)
    ids = lax.broadcasted_iota(jnp.int32, (n_experts, rows), 0) ^ me_ref[0]
    named0 = exp_ref[0:1, :] == ids
    named1 = exp_ref[1:2, :] == ids
    named = named0 | named1
    w_of = jnp.where(named0, weight[0:1, :], 0.0) + jnp.where(named1, weight[1:2, :], 0.0)
    position = contract(jnp.where(named, 1.0, 0.0).astype(BF16), jnp.where(earlier, 1.0, 0.0).astype(BF16), 1, 0)
    position = jnp.where(named, position, -1.0)
    slots = lax.broadcasted_iota(jnp.int32, (capacity, rows), 0).astype(F32)
    for k in range(n_experts):
        hit = slots == position[k : k + 1, :]
        table = jnp.where(hit, 1.0, 0.0).astype(BF16)
        table_w = jnp.where(hit, w_of[k : k + 1, :], 0.0).astype(BF16)
        table_ref[k * capacity : (k + 1) * capacity, :] = table
        messages[k][0:capacity, :] = contract(table, tok_ref[...], 1, 0).astype(BF16)
        messages[k][capacity:, :] = contract(table_w, cot_ref[...], 1, 0).astype(BF16)


def grad_kernel(n_msgs, n_own, capacity, *refs):
    msgs = refs[:n_msgs]
    wg_refs, wu_refs, wd_refs = refs[n_msgs : n_msgs + 2], refs[n_msgs + 2 : n_msgs + 4], refs[n_msgs + 4 : n_msgs + 6]
    outs = refs[n_msgs + 6 :]
    back, (da_ref, db_ref, h_ref) = outs[:-3], outs[-3:]
    width = msgs[0].shape[1]
    x = jnp.concatenate([m[0:capacity, :] for m in msgs], axis=0)
    gw = jnp.concatenate([m[capacity:, :] for m in msgs], axis=0)
    part_x = None
    part_g = None
    for q in range(2):
        a = contract(x, wg_refs[q][...], 1, 0)
        b = contract(x, wu_refs[q][...], 1, 0)
        dh = contract(gw, wd_refs[q][...], 1, 1)
        sig = 1.0 / (1.0 + jnp.exp(-a))
        act = a * sig
        h = act * b
        da = (dh * b * sig * (1.0 + a * (1.0 - sig))).astype(BF16)
        db = (dh * act).astype(BF16)
        hidden = a.shape[1]
        cols = slice(q * hidden, (q + 1) * hidden)
        da_ref[:, cols] = da
        db_ref[:, cols] = db
        h_ref[:, cols] = h.astype(BF16)
        px = contract(da, wg_refs[q][...], 1, 1) + contract(db, wu_refs[q][...], 1, 1)
        pg = jnp.sum(h * dh, axis=1, keepdims=True)
        part_x = px if part_x is None else part_x + px
        part_g = pg if part_g is None else part_g + pg
    n_rows = n_own * capacity
    for p in range(n_msgs // n_own):
        rows = slice(p * n_rows, (p + 1) * n_rows)
        back[p][:, 0:width] = part_x[rows, :].astype(BF16)
        back[p][:, width:] = jnp.broadcast_to(part_g[rows, :], (n_rows, LANES)).astype(BF16)


def weight_kernel(counts, capacity, quarter, has_received, *refs):
    n_msgs = sum(counts)
    msgs, refs = refs[:n_msgs], refs[n_msgs:]
    das, refs = refs[: len(counts)], refs[len(counts) :]
    dbs, refs = refs[: len(counts)], refs[len(counts) :]
    hs, refs = refs[: len(counts)], refs[len(counts) :]
    received, outs = (refs[:3], refs[3:]) if has_received else (None, refs)
    hidden = outs[2].shape[0]
    cols = slice(quarter * hidden, (quarter + 1) * hidden)
    x = jnp.concatenate([m[0:capacity, :] for m in msgs], axis=0)
    gw = jnp.concatenate([m[capacity:, :] for m in msgs], axis=0)
    da = jnp.concatenate([r[:, cols] for r in das], axis=0)
    db = jnp.concatenate([r[:, cols] for r in dbs], axis=0)
    h = jnp.concatenate([r[:, cols] for r in hs], axis=0)
    results = (contract(x, da, 0, 0), contract(x, db, 0, 0), contract(h, gw, 0, 0))
    for i in range(3):
        total = results[i]
        if has_received:
            total = total + received[i][...].astype(F32)
        outs[i][...] = total.astype(BF16)


def sum_kernel(n_parts, capacity, *refs):
    total = refs[0][...].astype(F32)
    for p in range(1, n_parts):
        total = total + refs[p][...].astype(F32)
    for m, out in enumerate(refs[n_parts:]):
        out[...] = total[m * capacity : (m + 1) * capacity, :].astype(BF16)


def combine_kernel(n_experts, capacity, me_ref, exp_ref, keep_ref, gate_ref, table_ref, *refs):
    msgs, (dtok_ref, dgate_ref) = refs[:n_experts], refs[n_experts:]
    width = dtok_ref.shape[1]
    rows = jnp.concatenate([m[:, 0:width] for m in msgs], axis=0)
    dtok_ref[...] = contract(table_ref[...], rows, 0, 0).astype(BF16)
    d_gates = jnp.zeros(exp_ref.shape, F32)
    for k in range(n_experts):
        value = contract(msgs[k][:, width:], table_ref[k * capacity : (k + 1) * capacity, :], 0, 0)
        d_gates = d_gates + jnp.where(exp_ref[...] == (me_ref[0] ^ k), value[0 : exp_ref.shape[0], :], 0.0)
    d_gates = d_gates * keep_ref[...].astype(F32) / gate_ref[...].astype(F32)
    dgate_ref[...] = d_gates.astype(BF16)


def call(body, outs, n_in, smem=0, cost=None):
    vmem = pl.BlockSpec(memory_space=pltpu.VMEM)
    scalar = pl.BlockSpec(memory_space=pltpu.SMEM)
    return pl.pallas_call(
        body,
        out_shape=[jax.ShapeDtypeStruct(shape, BF16) for shape in outs],
        in_specs=[scalar] * smem + [vmem] * (n_in - smem),
        out_specs=[vmem] * len(outs),
        cost_estimate=cost,
        compiler_params=pltpu.CompilerParams(vmem_limit_bytes=VMEM_LIMIT),
    )


def groups_of(n_experts):
    half = n_experts // 2
    groups = ([0, 1, half], [k for k in range(2, half)] + [half + 1], list(range(half + 2, n_experts)))
    return {f"g{i}": g for i, g in enumerate(groups) if g}


def local_tiled(tokens, cotangent, gates, experts, keep, gate_w, up_w, down_w):
    return local_steps(tokens, cotangent, gates, experts, keep, gate_w, up_w, down_w)


def local_steps(tokens, cotangent, gates, experts, keep, gate_w, up_w, down_w):
    n_experts = lax.axis_size("ep")
    n_groups = lax.axis_size("zr")
    tok_rows, width = tokens.shape
    hidden = gate_w.shape[2]
    capacity = 3 * tok_rows // n_experts
    me = lax.axis_index("ep").astype(jnp.int32).reshape(1)
    route = (me, experts.T, keep.T, gates.T)

    def exchange(value, axis, size, bit):
        return lax.ppermute(value, axis, [(i, i ^ bit) for i in range(size)])

    def run(body, outs, *args, smem=0):
        return call(body, outs, len(args), smem=smem)(*args)

    weights = []
    for w in (gate_w, up_w, down_w):
        weights += [w[0], exchange(w[0], "zr", n_groups, 1)]

    outs = [(n_experts * capacity, tok_rows)] + [(2 * capacity, width)] * n_experts
    table, *sends = run(functools.partial(send_kernel, n_experts, capacity), outs, *route, tokens, cotangent, smem=1)
    mine = [exchange(sends[k], "ep", n_experts, k) if k else sends[0] for k in range(n_experts)]
    peers = list(range(2, n_groups, 2))
    theirs = [[exchange(mine[k], "zr", n_groups, r) for r in peers] for k in range(n_experts)]

    all_msgs, counts, das, dbs, hs, returned = [], [], [], [], [], {}
    for group in groups_of(n_experts).values():
        msgs = [mine[k] for k in group] + [theirs[k][p] for p in range(len(peers)) for k in group]
        n_rows, n_own = len(msgs) * capacity, len(group) * capacity
        outs = [(n_own, width + LANES)] * (1 + len(peers)) + [(n_rows, 2 * hidden)] * 3
        body = functools.partial(grad_kernel, len(msgs), len(group), capacity)
        *back, da, db, h = run(body, outs, *msgs, *weights)
        all_msgs, counts = all_msgs + msgs, counts + [len(msgs)]
        das, dbs, hs = das + [da], dbs + [db], hs + [h]
        parts = [back[0]] + [exchange(back[1 + p], "zr", n_groups, r) for p, r in enumerate(peers)]
        body = functools.partial(sum_kernel, len(parts), capacity)
        summed = run(body, [(capacity, width + LANES)] * len(group), *parts)
        for i, k in enumerate(group):
            returned[k] = exchange(summed[i], "ep", n_experts, k) if k else summed[i]

    w_outs = [(width, hidden), (width, hidden), (hidden, width)]
    w_args = all_msgs + das + dbs + hs
    partner = run(functools.partial(weight_kernel, counts, capacity, 1, False), w_outs, *w_args)
    w_args = w_args + [exchange(w, "zr", n_groups, 1) for w in partner]
    dwg, dwu, dwd = run(functools.partial(weight_kernel, counts, capacity, 0, True), w_outs, *w_args)

    outs = [(tok_rows, width), experts.T.shape]
    d_tokens, d_gates = run(
        functools.partial(combine_kernel, n_experts, capacity),
        outs,
        *route,
        table,
        *[returned[k] for k in range(n_experts)],
        smem=1,
    )
    return d_tokens, d_gates.T, dwg[None], dwu[None], dwd[None]


def route_tables(experts, keep, gates, n_experts, capacity):
    tok_rows = experts.shape[0]
    flat_exp = experts.reshape(-1)
    onehot = (flat_exp[:, None] == jnp.arange(n_experts, dtype=jnp.int32)[None, :]).astype(
        jnp.int32
    )
    before = jnp.cumsum(onehot, axis=0) - onehot
    position = jnp.sum(before * onehot, axis=1)
    dest = (flat_exp * capacity + position).reshape(tok_rows, 2)
    slot_ids = jnp.arange(n_experts * capacity, dtype=jnp.int32)
    matches = dest[None, :, :] == slot_ids[:, None, None]
    table = jnp.any(matches, axis=2).astype(jnp.bfloat16)
    weight = gates.astype(jnp.float32) * keep.astype(jnp.float32)
    slot_weight = jnp.sum(jnp.where(matches, weight[None, :, :], 0.0), axis=(1, 2))
    return (table, dest, slot_weight)


def expert_grads(slot_input_rows, slot_g, slot_w, wg, wu, wd):
    pre_a = jnp.dot(slot_input_rows, wg, preferred_element_type=jnp.float32)
    pre_b = jnp.dot(slot_input_rows, wu, preferred_element_type=jnp.float32)
    sig = 1.0 / (1.0 + jnp.exp(-pre_a))
    act = pre_a * sig
    hidden_activation = act * pre_b
    value_gradient = jnp.einsum("sd,hd->sh", slot_g, wd, preferred_element_type=jnp.float32)
    scale = slot_w.astype(jnp.float32)[:, None]
    dh = scale * value_gradient
    gate_branch_gradient = (dh * pre_b * sig * (1.0 + pre_a * (1.0 - sig))).astype(jnp.bfloat16)
    up_branch_gradient = (dh * act).astype(jnp.bfloat16)
    hidden_w = (scale * hidden_activation).astype(jnp.bfloat16)
    dwg = jnp.einsum(
        "sd,sh->dh", slot_input_rows, gate_branch_gradient, preferred_element_type=jnp.float32
    ).astype(jnp.bfloat16)
    dwu = jnp.einsum(
        "sd,sh->dh", slot_input_rows, up_branch_gradient, preferred_element_type=jnp.float32
    ).astype(jnp.bfloat16)
    dwd = jnp.einsum("sh,sd->hd", hidden_w, slot_g, preferred_element_type=jnp.float32).astype(
        jnp.bfloat16
    )
    part_x = jnp.einsum("sh,dh->sd", gate_branch_gradient, wg, preferred_element_type=jnp.float32)
    part_x = part_x + jnp.einsum(
        "sh,dh->sd", up_branch_gradient, wu, preferred_element_type=jnp.float32
    )
    partial_gate_rows = jnp.sum(hidden_activation * value_gradient, axis=1)
    return (dwg, dwu, dwd, part_x.astype(jnp.bfloat16), partial_gate_rows.astype(jnp.bfloat16))


def local_general(tokens, cotangent, gates, experts, keep, gate_w, up_w, down_w):
    n_experts = lax.axis_size("ep")
    n_groups = lax.axis_size("zr")
    tok_rows = tokens.shape[0]
    width = tokens.shape[1]
    capacity = max(2, 3 * tok_rows // n_experts)
    flat_width = capacity * width
    table, dest, slot_weight = route_tables(experts, keep, gates, n_experts, capacity)
    send_x = jnp.dot(table, tokens, preferred_element_type=jnp.float32).astype(jnp.bfloat16)
    send_g = jnp.dot(table, cotangent, preferred_element_type=jnp.float32).astype(jnp.bfloat16)
    send_x = send_x.reshape(1, n_experts, flat_width)
    send_g = send_g.reshape(1, n_experts, flat_width)
    send_w = slot_weight.astype(jnp.bfloat16).reshape(1, n_experts, capacity)
    moved = (
        lax.all_to_all(send_x, "ep", split_axis=1, concat_axis=1, tiled=True),
        lax.all_to_all(send_g, "ep", split_axis=1, concat_axis=1, tiled=True),
        lax.all_to_all(send_w, "ep", split_axis=1, concat_axis=1, tiled=True),
    )
    arrived = (
        lax.all_gather(moved[0], "zr", axis=0, tiled=True),
        lax.all_gather(moved[1], "zr", axis=0, tiled=True),
        lax.all_gather(moved[2], "zr", axis=0, tiled=True),
    )
    slot_input_rows = arrived[0].reshape(-1, width)
    slot_g = arrived[1].reshape(-1, width)
    slot_w = arrived[2].reshape(-1)
    dwg, dwu, dwd, part_x, partial_gate_rows = expert_grads(
        slot_input_rows, slot_g, slot_w, gate_w[0], up_w[0], down_w[0]
    )
    part_x = part_x.reshape(n_groups, n_experts, flat_width)
    partial_gate_rows = partial_gate_rows.reshape(n_groups, n_experts, capacity)
    summed = (
        lax.psum_scatter(
            part_x.astype(jnp.float32).astype(jnp.bfloat16), "zr", scatter_dimension=0, tiled=True
        ).astype(jnp.float32),
        lax.psum_scatter(
            partial_gate_rows.astype(jnp.float32).astype(jnp.bfloat16),
            "zr",
            scatter_dimension=0,
            tiled=True,
        ).astype(jnp.float32),
    )
    rounded = (summed[0].astype(jnp.bfloat16), summed[1].astype(jnp.bfloat16))
    returned = (
        lax.all_to_all(rounded[0], "ep", split_axis=1, concat_axis=1, tiled=True),
        lax.all_to_all(rounded[1], "ep", split_axis=1, concat_axis=1, tiled=True),
    )
    slot_dx = returned[0]
    slot_dg = returned[1]
    slot_dx = slot_dx.reshape(n_experts * capacity, width)
    slot_dg = slot_dg.reshape(n_experts * capacity)
    d_tokens = jnp.einsum("st,sd->td", table, slot_dx, preferred_element_type=jnp.float32).astype(
        jnp.bfloat16
    )
    d_gates = jnp.take(slot_dg, dest) * keep.astype(jnp.bfloat16)
    return (d_tokens, d_gates, dwg[None], dwu[None], dwd[None])


def paired(mesh):
    counts = (mesh.shape["ep"], mesh.shape["zr"])
    return all(c > 2 and c & (c - 1) == 0 for c in counts)


def tiled(mesh, tokens):
    n_experts, n_groups = mesh.shape["ep"], mesh.shape["zr"]
    capacity = 3 * (tokens.shape[0] // (n_experts * n_groups)) // n_experts
    return paired(mesh) and capacity % 16 == 0 and tokens.shape[1] % LANES == 0


def solution(mesh):
    placed = (
        P(("ep", "zr"), None),
        P(("ep", "zr"), None),
        P(("ep", "zr"), None),
        P(("ep", "zr"), None),
        P(("ep", "zr"), None),
        P("ep", None, "zr"),
        P("ep", None, "zr"),
        P("ep", "zr", None),
    )

    def sharded(local):
        return jax.shard_map(
            local,
            mesh=mesh,
            in_specs=placed,
            out_specs=(
                P(("ep", "zr"), None),
                P(("ep", "zr"), None),
                P("ep", None, "zr"),
                P("ep", None, "zr"),
                P("ep", "zr", None),
            ),
            check_vma=False,
        )

    def step(tokens, *rest):
        chosen = local_tiled if tiled(mesh, tokens) else local_general
        return sharded(chosen)(tokens, *rest)

    return step
```

```python
import functools

import jax
import jax.numpy as jnp
from jax import lax
from jax.experimental import pallas as pl
from jax.experimental.pallas import tpu as pltpu
from jax.sharding import PartitionSpec as P


F32 = jnp.float32
BF16 = jnp.bfloat16
LANES = 128
SUBLANES = 8
VMEM_LIMIT = 24 * 1024 * 1024


def contract(a, b, dim_a, dim_b):
    return lax.dot_general(a, b, (((dim_a,), (dim_b,)), ((), ())), preferred_element_type=F32)


def fetch(sources, targets, sems):
    copies = [pltpu.make_async_copy(a, b, sems.at[i]) for i, (a, b) in enumerate(zip(sources, targets))]
    for copy in copies:
        copy.start()
    return copies


def send_kernel(n_experts, capacity, me_ref, *refs):
    sources, refs = refs[:5], refs[5:]
    (table_ref, exp_out, ratio_out), refs = refs[:3], refs[3:]
    messages, (exp_ref, keep_ref, gate_ref, tok_ref, cot_ref, sems) = refs[:n_experts], refs[n_experts:]
    copies = fetch(sources, (exp_ref, keep_ref, gate_ref, tok_ref, cot_ref), sems)
    rows = tok_ref.shape[0]
    earlier = lax.broadcasted_iota(jnp.int32, (rows, rows), 0) < lax.broadcasted_iota(jnp.int32, (rows, rows), 1)
    ids = lax.broadcasted_iota(jnp.int32, (n_experts, rows), 0) ^ me_ref[0]
    for copy in copies[:3]:
        copy.wait()
    gate = gate_ref[...].astype(F32)
    keep = keep_ref[...].astype(F32)
    weight = gate * keep
    exp_out[...] = exp_ref[...]
    ratio_out[...] = keep / gate
    named0 = exp_ref[0:1, :] == ids
    named1 = exp_ref[1:2, :] == ids
    named = named0 | named1
    w_of = jnp.where(named0, weight[0:1, :], 0.0) + jnp.where(named1, weight[1:2, :], 0.0)
    position = contract(jnp.where(named, 1.0, 0.0).astype(BF16), jnp.where(earlier, 1.0, 0.0).astype(BF16), 1, 0)
    position = jnp.where(named, position, -1.0)
    slots = lax.broadcasted_iota(jnp.int32, (capacity, rows), 0).astype(F32)
    for copy in copies[3:]:
        copy.wait()
    for k in range(n_experts):
        hit = slots == position[k : k + 1, :]
        table = jnp.where(hit, 1.0, 0.0).astype(BF16)
        table_w = jnp.where(hit, w_of[k : k + 1, :], 0.0).astype(BF16)
        table_ref[k * capacity : (k + 1) * capacity, :] = table
        messages[k][0:capacity, :] = contract(table, tok_ref[...], 1, 0).astype(BF16)
        messages[k][capacity:, :] = contract(table_w, cot_ref[...], 1, 0).astype(BF16)


def stage_kernel(*refs):
    for copy in fetch(refs[:3], refs[3:6], refs[6]):
        copy.wait()


def pack(target, m, capacity, values, sums):
    blocks = values.shape[1] // LANES
    base = m * (blocks * capacity + SUBLANES)
    for j in range(blocks):
        target[base + j * capacity : base + (j + 1) * capacity, :] = values[:, j * LANES : (j + 1) * LANES].astype(BF16)
    tail = slice(base + blocks * capacity, base + blocks * capacity + SUBLANES)
    target[tail, :] = jnp.zeros((SUBLANES, LANES), BF16)
    target[tail, 0:capacity] = sums.astype(BF16)


def grad_kernel(n_parts, chunks, capacity, *refs):
    n_own = sum(chunks)
    n_msgs = n_parts * n_own
    msgs = refs[:n_msgs]
    wg_refs, wu_refs, wd_refs = refs[n_msgs : n_msgs + 2], refs[n_msgs + 2 : n_msgs + 4], refs[n_msgs + 4 : n_msgs + 6]
    outs = refs[n_msgs + 6 :]
    back, (da_ref, db_ref, h_ref) = outs[:-3], outs[-3:]
    x = jnp.concatenate([m[0:capacity, :] for m in msgs], axis=0)
    gw = jnp.concatenate([m[capacity:, :] for m in msgs], axis=0)
    part_x = None
    part_g = None
    for q in range(2):
        a = contract(x, wg_refs[q][...], 1, 0)
        b = contract(x, wu_refs[q][...], 1, 0)
        dh = contract(gw, wd_refs[q][...], 1, 1)
        sig = 1.0 / (1.0 + jnp.exp(-a))
        act = a * sig
        h = act * b
        da = (dh * b * sig * (1.0 + a * (1.0 - sig))).astype(BF16)
        db = (dh * act).astype(BF16)
        hidden = a.shape[1]
        cols = slice(q * hidden, (q + 1) * hidden)
        da_ref[:, cols] = da
        db_ref[:, cols] = db
        h_ref[:, cols] = h.astype(BF16)
        px = contract(da, wg_refs[q][...], 1, 1) + contract(db, wu_refs[q][...], 1, 1)
        pg = h * dh
        part_x = px if part_x is None else part_x + px
        part_g = pg if part_g is None else part_g + pg
    high = part_g.astype(BF16)
    low = (part_g - high.astype(F32)).astype(BF16)
    ones = jnp.ones((SUBLANES, part_g.shape[1]), BF16)
    m = 0
    for target in [back[p * len(chunks) + c] for p in range(n_parts) for c in range(len(chunks))]:
        count = target.shape[0] // (part_x.shape[1] // LANES * capacity + SUBLANES)
        for i in range(count):
            rows = slice(m * capacity, (m + 1) * capacity)
            sums = contract(ones, high[rows, :], 1, 1) + contract(ones, low[rows, :], 1, 1)
            pack(target, i, capacity, part_x[rows, :], sums)
            m += 1


def weight_kernel(counts, capacity, quarter, *refs):
    n_msgs = sum(counts)
    msgs, refs = refs[:n_msgs], refs[n_msgs:]
    das, refs = refs[: len(counts)], refs[len(counts) :]
    dbs, refs = refs[: len(counts)], refs[len(counts) :]
    hs, outs = refs[: len(counts)], refs[len(counts) :]
    hidden = outs[2].shape[0]
    cols = slice(quarter * hidden, (quarter + 1) * hidden)
    x = jnp.concatenate([m[0:capacity, :] for m in msgs], axis=0)
    gw = jnp.concatenate([m[capacity:, :] for m in msgs], axis=0)
    da = jnp.concatenate([r[:, cols] for r in das], axis=0)
    db = jnp.concatenate([r[:, cols] for r in dbs], axis=0)
    h = jnp.concatenate([r[:, cols] for r in hs], axis=0)
    for out, total in zip(outs, (contract(x, da, 0, 0), contract(x, db, 0, 0), contract(h, gw, 0, 0))):
        out[...] = total.astype(out.dtype)


def add_kernel(*refs):
    for own, received, out in zip(refs[:3], refs[3:6], refs[6:]):
        out[...] = (own[...] + received[...].astype(F32)).astype(BF16)


def sum_kernel(n_parts, *refs):
    outs = refs[n_parts:]
    total = refs[0][...].astype(F32)
    for part in refs[1:n_parts]:
        total = total + part[...].astype(F32)
    rows = total.shape[0] // len(outs)
    for i, out in enumerate(outs):
        out[...] = total[i * rows : (i + 1) * rows, :].astype(BF16)


def combine_kernel(n_experts, capacity, me_ref, exp_ref, ratio_ref, table_ref, *refs):
    msgs, (dtok_ref, dgate_ref) = refs[:n_experts], refs[n_experts:]
    blocks = dtok_ref.shape[1] // LANES
    rows = []
    for m in msgs:
        rows.append(jnp.concatenate([m[j * capacity : (j + 1) * capacity, :] for j in range(blocks)], axis=1))
    dtok_ref[...] = contract(table_ref[...], jnp.concatenate(rows, axis=0), 0, 0).astype(BF16)
    d_gates = jnp.zeros(exp_ref.shape, F32)
    for k in range(n_experts):
        sums = msgs[k][blocks * capacity :, 0:capacity]
        value = contract(sums, table_ref[k * capacity : (k + 1) * capacity, :], 1, 0)
        d_gates = d_gates + jnp.where(exp_ref[...] == (me_ref[0] ^ k), value[0 : exp_ref.shape[0], :], 0.0)
    dgate_ref[...] = (d_gates * ratio_ref[...]).astype(BF16)


def call(body, outs, n_in, smem=0, hbm=0, scratch=()):
    def spec(space):
        return pl.BlockSpec(memory_space=space)

    outs = [out if isinstance(out, jax.ShapeDtypeStruct) else jax.ShapeDtypeStruct(out, BF16) for out in outs]
    return pl.pallas_call(
        body,
        out_shape=outs,
        in_specs=[spec(pltpu.SMEM)] * smem
        + [spec(pltpu.HBM)] * hbm
        + [spec(pltpu.VMEM)] * (n_in - smem - hbm),
        out_specs=[spec(pltpu.VMEM)] * len(outs),
        scratch_shapes=list(scratch),
        compiler_params=pltpu.CompilerParams(vmem_limit_bytes=VMEM_LIMIT),
    )


def chunks_of(n_experts):
    size = n_experts // 4
    return [list(range(i * size, (i + 1) * size)) for i in range(4)]


def groups_of(n_experts):
    first, second, third, fourth = chunks_of(n_experts)
    return [[first, second], [third], [fourth]]


def local_tiled(tokens, cotangent, gates, experts, keep, gate_w, up_w, down_w):
    return local_steps(tokens, cotangent, gates, experts, keep, gate_w, up_w, down_w)


def local_steps(tokens, cotangent, gates, experts, keep, gate_w, up_w, down_w):
    n_experts = lax.axis_size("ep")
    n_groups = lax.axis_size("zr")
    tok_rows, width = tokens.shape
    hidden = gate_w.shape[2]
    capacity = 3 * tok_rows // n_experts
    me = lax.axis_index("ep").astype(jnp.int32).reshape(1)
    route = (experts.T, keep.T, gates.T)

    def exchange(value, axis, size, bit):
        return lax.ppermute(value, axis, [(i, i ^ bit) for i in range(size)])

    def run(body, outs, *args, **kinds):
        return call(body, outs, len(args), **kinds)(*args)

    held = [pltpu.with_memory_space_constraint(w[0], pltpu.HBM) for w in (gate_w, up_w, down_w)]
    swapped = [exchange(w[0], "zr", n_groups, 1) for w in (gate_w, up_w, down_w)]
    sems = pltpu.SemaphoreType.DMA
    held = run(stage_kernel, [w.shape for w in held], *held, hbm=3, scratch=[sems((3,))])
    weights = [w for pair in zip(held, swapped) for w in pair]

    inputs = [pltpu.with_memory_space_constraint(v, pltpu.HBM) for v in (*route, tokens, cotangent)]
    outs = [(n_experts * capacity, tok_rows), jax.ShapeDtypeStruct(route[0].shape, jnp.int32)]
    outs += [jax.ShapeDtypeStruct(route[0].shape, F32)] + [(2 * capacity, width)] * n_experts
    table, named, ratio, *sends = run(
        functools.partial(send_kernel, n_experts, capacity),
        outs,
        me,
        *inputs,
        smem=1,
        hbm=len(inputs),
        scratch=[pltpu.VMEM(v.shape, v.dtype) for v in inputs] + [sems((len(inputs),))],
    )
    mine = [exchange(sends[k], "ep", n_experts, k) if k else sends[0] for k in range(n_experts)]
    peers = list(range(2, n_groups, 2))
    theirs = [[exchange(mine[k], "zr", n_groups, r) for r in peers] for k in range(n_experts)]

    n_parts = 1 + len(peers)
    msg_rows = width // LANES * capacity + SUBLANES
    all_msgs, counts, das, dbs, hs, returned = [], [], [], [], [], {}
    for chunks in groups_of(n_experts):
        group = sum(chunks, [])
        msgs = [mine[k] for k in group] + [theirs[k][p] for p in range(len(peers)) for k in group]
        outs = [(len(chunk) * msg_rows, LANES) for chunk in chunks] * n_parts
        outs += [(len(msgs) * capacity, 2 * hidden)] * 3
        body = functools.partial(grad_kernel, n_parts, [len(chunk) for chunk in chunks], capacity)
        *back, da, db, h = run(body, outs, *msgs, *weights)
        all_msgs, counts = all_msgs + msgs, counts + [len(msgs)]
        das, dbs, hs = das + [da], dbs + [db], hs + [h]
        for c, chunk in enumerate(chunks):
            parts = [back[c]]
            for p, r in enumerate(peers):
                parts.append(exchange(back[(p + 1) * len(chunks) + c], "zr", n_groups, r))
            body = functools.partial(sum_kernel, n_parts)
            summed = run(body, [(msg_rows, LANES)] * len(chunk), *parts)
            for k, value in zip(chunk, summed):
                returned[k] = exchange(value, "ep", n_experts, k) if k else value

    shapes = [(width, hidden), (width, hidden), (hidden, width)]
    w_args = all_msgs + das + dbs + hs
    partner = run(functools.partial(weight_kernel, counts, capacity, 1), shapes, *w_args)
    received = [exchange(w, "zr", n_groups, 1) for w in partner]
    own = run(
        functools.partial(weight_kernel, counts, capacity, 0),
        [jax.ShapeDtypeStruct(shape, F32) for shape in shapes],
        *w_args,
    )
    dwg, dwu, dwd = run(add_kernel, shapes, *own, *received)

    outs = [(tok_rows, width), experts.T.shape]
    d_tokens, d_gates = run(
        functools.partial(combine_kernel, n_experts, capacity),
        outs,
        me,
        named,
        ratio,
        table,
        *[returned[k] for k in range(n_experts)],
        smem=1,
    )
    return d_tokens, d_gates.T, dwg[None], dwu[None], dwd[None]


def route_tables(experts, keep, gates, n_experts, capacity):
    tok_rows = experts.shape[0]
    flat_exp = experts.reshape(-1)
    onehot = (flat_exp[:, None] == jnp.arange(n_experts, dtype=jnp.int32)[None, :]).astype(
        jnp.int32
    )
    before = jnp.cumsum(onehot, axis=0) - onehot
    position = jnp.sum(before * onehot, axis=1)
    dest = (flat_exp * capacity + position).reshape(tok_rows, 2)
    slot_ids = jnp.arange(n_experts * capacity, dtype=jnp.int32)
    matches = dest[None, :, :] == slot_ids[:, None, None]
    table = jnp.any(matches, axis=2).astype(jnp.bfloat16)
    weight = gates.astype(jnp.float32) * keep.astype(jnp.float32)
    slot_weight = jnp.sum(jnp.where(matches, weight[None, :, :], 0.0), axis=(1, 2))
    return (table, dest, slot_weight)


def expert_grads(slot_input_rows, slot_g, slot_w, wg, wu, wd):
    pre_a = jnp.dot(slot_input_rows, wg, preferred_element_type=jnp.float32)
    pre_b = jnp.dot(slot_input_rows, wu, preferred_element_type=jnp.float32)
    sig = 1.0 / (1.0 + jnp.exp(-pre_a))
    act = pre_a * sig
    hidden_activation = act * pre_b
    value_gradient = jnp.einsum("sd,hd->sh", slot_g, wd, preferred_element_type=jnp.float32)
    scale = slot_w.astype(jnp.float32)[:, None]
    dh = scale * value_gradient
    gate_branch_gradient = (dh * pre_b * sig * (1.0 + pre_a * (1.0 - sig))).astype(jnp.bfloat16)
    up_branch_gradient = (dh * act).astype(jnp.bfloat16)
    hidden_w = (scale * hidden_activation).astype(jnp.bfloat16)
    dwg = jnp.einsum(
        "sd,sh->dh", slot_input_rows, gate_branch_gradient, preferred_element_type=jnp.float32
    ).astype(jnp.bfloat16)
    dwu = jnp.einsum(
        "sd,sh->dh", slot_input_rows, up_branch_gradient, preferred_element_type=jnp.float32
    ).astype(jnp.bfloat16)
    dwd = jnp.einsum("sh,sd->hd", hidden_w, slot_g, preferred_element_type=jnp.float32).astype(
        jnp.bfloat16
    )
    part_x = jnp.einsum("sh,dh->sd", gate_branch_gradient, wg, preferred_element_type=jnp.float32)
    part_x = part_x + jnp.einsum(
        "sh,dh->sd", up_branch_gradient, wu, preferred_element_type=jnp.float32
    )
    partial_gate_rows = jnp.sum(hidden_activation * value_gradient, axis=1)
    return (dwg, dwu, dwd, part_x.astype(jnp.bfloat16), partial_gate_rows.astype(jnp.bfloat16))


def local_general(tokens, cotangent, gates, experts, keep, gate_w, up_w, down_w):
    n_experts = lax.axis_size("ep")
    n_groups = lax.axis_size("zr")
    tok_rows = tokens.shape[0]
    width = tokens.shape[1]
    capacity = max(2, 3 * tok_rows // n_experts)
    flat_width = capacity * width
    table, dest, slot_weight = route_tables(experts, keep, gates, n_experts, capacity)
    send_x = jnp.dot(table, tokens, preferred_element_type=jnp.float32).astype(jnp.bfloat16)
    send_g = jnp.dot(table, cotangent, preferred_element_type=jnp.float32).astype(jnp.bfloat16)
    send_x = send_x.reshape(1, n_experts, flat_width)
    send_g = send_g.reshape(1, n_experts, flat_width)
    send_w = slot_weight.astype(jnp.bfloat16).reshape(1, n_experts, capacity)
    moved = (
        lax.all_to_all(send_x, "ep", split_axis=1, concat_axis=1, tiled=True),
        lax.all_to_all(send_g, "ep", split_axis=1, concat_axis=1, tiled=True),
        lax.all_to_all(send_w, "ep", split_axis=1, concat_axis=1, tiled=True),
    )
    arrived = (
        lax.all_gather(moved[0], "zr", axis=0, tiled=True),
        lax.all_gather(moved[1], "zr", axis=0, tiled=True),
        lax.all_gather(moved[2], "zr", axis=0, tiled=True),
    )
    slot_input_rows = arrived[0].reshape(-1, width)
    slot_g = arrived[1].reshape(-1, width)
    slot_w = arrived[2].reshape(-1)
    dwg, dwu, dwd, part_x, partial_gate_rows = expert_grads(
        slot_input_rows, slot_g, slot_w, gate_w[0], up_w[0], down_w[0]
    )
    part_x = part_x.reshape(n_groups, n_experts, flat_width)
    partial_gate_rows = partial_gate_rows.reshape(n_groups, n_experts, capacity)
    summed = (
        lax.psum_scatter(
            part_x.astype(jnp.float32).astype(jnp.bfloat16), "zr", scatter_dimension=0, tiled=True
        ).astype(jnp.float32),
        lax.psum_scatter(
            partial_gate_rows.astype(jnp.float32).astype(jnp.bfloat16),
            "zr",
            scatter_dimension=0,
            tiled=True,
        ).astype(jnp.float32),
    )
    rounded = (summed[0].astype(jnp.bfloat16), summed[1].astype(jnp.bfloat16))
    returned = (
        lax.all_to_all(rounded[0], "ep", split_axis=1, concat_axis=1, tiled=True),
        lax.all_to_all(rounded[1], "ep", split_axis=1, concat_axis=1, tiled=True),
    )
    slot_dx = returned[0]
    slot_dg = returned[1]
    slot_dx = slot_dx.reshape(n_experts * capacity, width)
    slot_dg = slot_dg.reshape(n_experts * capacity)
    d_tokens = jnp.einsum("st,sd->td", table, slot_dx, preferred_element_type=jnp.float32).astype(
        jnp.bfloat16
    )
    d_gates = jnp.take(slot_dg, dest) * keep.astype(jnp.bfloat16)
    return (d_tokens, d_gates, dwg[None], dwu[None], dwd[None])


def paired(mesh):
    counts = (mesh.shape["ep"], mesh.shape["zr"])
    return all(c > 2 and c & (c - 1) == 0 for c in counts)


def tiled(mesh, tokens):
    n_experts, n_groups = mesh.shape["ep"], mesh.shape["zr"]
    capacity = 3 * (tokens.shape[0] // (n_experts * n_groups)) // n_experts
    return paired(mesh) and capacity % 16 == 0 and tokens.shape[1] % LANES == 0


def solution(mesh):
    placed = (
        P(("ep", "zr"), None),
        P(("ep", "zr"), None),
        P(("ep", "zr"), None),
        P(("ep", "zr"), None),
        P(("ep", "zr"), None),
        P("ep", None, "zr"),
        P("ep", None, "zr"),
        P("ep", "zr", None),
    )

    def sharded(local):
        return jax.shard_map(
            local,
            mesh=mesh,
            in_specs=placed,
            out_specs=(
                P(("ep", "zr"), None),
                P(("ep", "zr"), None),
                P("ep", None, "zr"),
                P("ep", None, "zr"),
                P("ep", "zr", None),
            ),
            check_vma=False,
        )

    def step(tokens, *rest):
        chosen = local_tiled if tiled(mesh, tokens) else local_general
        return sharded(chosen)(tokens, *rest)

    return step
```

```python
import functools

import jax
import jax.numpy as jnp
from jax import lax
from jax.experimental import pallas as pl
from jax.experimental.pallas import tpu as pltpu
from jax.sharding import PartitionSpec as P


F32 = jnp.float32
BF16 = jnp.bfloat16
LANES = 128
SUBLANES = 8
VMEM_LIMIT = 24 * 1024 * 1024


def contract(a, b, dim_a, dim_b):
    return lax.dot_general(a, b, (((dim_a,), (dim_b,)), ((), ())), preferred_element_type=F32)


def fetch(sources, targets, sems):
    copies = [pltpu.make_async_copy(a, b, sems.at[i]) for i, (a, b) in enumerate(zip(sources, targets))]
    for copy in copies:
        copy.start()
    return copies


def slot_tables(experts, ids, capacity):
    rows = experts.shape[1]
    earlier = lax.broadcasted_iota(jnp.int32, (rows, rows), 0) < lax.broadcasted_iota(jnp.int32, (rows, rows), 1)
    named = (experts[0:1, :] == ids) | (experts[1:2, :] == ids)
    position = contract(jnp.where(named, 1.0, 0.0).astype(BF16), jnp.where(earlier, 1.0, 0.0).astype(BF16), 1, 0)
    position = jnp.where(named, position, -1.0)
    slots = lax.broadcasted_iota(jnp.int32, (capacity, rows), 0).astype(F32)
    return [slots == position[k : k + 1, :] for k in range(ids.shape[0])]


def partner_ids(count, rows, me):
    return lax.broadcasted_iota(jnp.int32, (count, rows), 0) ^ me


def send_kernel(n_experts, capacity, me_ref, *refs):
    sources, refs = refs[:5], refs[5:]
    (table_ref, exp_out, ratio_out, route_out), refs = refs[:4], refs[4:]
    messages, (exp_ref, keep_ref, gate_ref, tok_ref, cot_ref, sems) = refs[:n_experts], refs[n_experts:]
    copies = fetch(sources, (exp_ref, keep_ref, gate_ref, tok_ref, cot_ref), sems)
    ids = partner_ids(n_experts, tok_ref.shape[0], me_ref[0])
    for copy in copies[:3]:
        copy.wait()
    gate = gate_ref[...].astype(F32)
    keep = keep_ref[...].astype(F32)
    experts = exp_ref[...]
    weight = gate * keep
    exp_out[...] = experts
    ratio_out[...] = keep / gate
    route_out[...] = jnp.zeros(route_out.shape, jnp.int32)
    route_out[0:2, :] = experts
    w_of = jnp.where(experts[0:1, :] == ids, weight[0:1, :], 0.0)
    w_of = w_of + jnp.where(experts[1:2, :] == ids, weight[1:2, :], 0.0)
    hits = slot_tables(experts, ids, capacity)
    for copy in copies[3:]:
        copy.wait()
    for k, hit in enumerate(hits):
        table = jnp.where(hit, 1.0, 0.0).astype(BF16)
        table_w = jnp.where(hit, w_of[k : k + 1, :], 0.0).astype(BF16)
        table_ref[k * capacity : (k + 1) * capacity, :] = table
        messages[k][0:capacity, :] = contract(table, tok_ref[...], 1, 0).astype(BF16)
        messages[k][capacity:, :] = contract(table_w, cot_ref[...], 1, 0).astype(BF16)


def stage_kernel(*refs):
    sources, (wg_ref, wu_ref), turned, (wd_ref, sems) = refs[:3], refs[3:5], refs[5:8], refs[8:]
    copies = fetch(sources, (wg_ref, wu_ref, wd_ref), sems)
    for copy, ref, out in zip(copies, (wg_ref, wu_ref, wd_ref), turned):
        copy.wait()
        out[...] = ref[...].T


def turn_kernel(*refs):
    for ref, out in zip(refs[:3], refs[3:]):
        out[...] = ref[...].T


def pack(target, m, capacity, values, sums):
    blocks = values.shape[1] // LANES
    base = m * (blocks * capacity + SUBLANES)
    for j in range(blocks):
        target[base + j * capacity : base + (j + 1) * capacity, :] = values[:, j * LANES : (j + 1) * LANES].astype(BF16)
    tail = slice(base + blocks * capacity, base + blocks * capacity + SUBLANES)
    target[tail, :] = jnp.zeros((SUBLANES, LANES), BF16)
    target[tail, 0:capacity] = sums.astype(BF16)


def grad_kernel(n_msgs, layout, capacity, *refs):
    msgs = refs[:n_msgs]
    weights, outs = (refs[n_msgs : n_msgs + 5], refs[n_msgs + 5 : n_msgs + 10]), refs[n_msgs + 10 :]
    back, (da_ref, db_ref, h_ref) = outs[:-3], outs[-3:]
    x = jnp.concatenate([m[0:capacity, :] for m in msgs], axis=0)
    gw = jnp.concatenate([m[capacity:, :] for m in msgs], axis=0)
    part_x = None
    part_g = None
    for q in range(2):
        wg, wu, wg_t, wu_t, wd_t = [ref[...] for ref in weights[q]]
        a = contract(x, wg, 1, 0)
        b = contract(x, wu, 1, 0)
        dh = contract(gw, wd_t, 1, 0)
        sig = 1.0 / (1.0 + jnp.exp(-a))
        act = a * sig
        h = act * b
        da = (dh * b * sig * (1.0 + a * (1.0 - sig))).astype(BF16)
        db = (dh * act).astype(BF16)
        hidden = a.shape[1]
        cols = slice(q * hidden, (q + 1) * hidden)
        da_ref[:, cols] = da
        db_ref[:, cols] = db
        h_ref[:, cols] = h.astype(BF16)
        px = contract(da, wg_t, 1, 0) + contract(db, wu_t, 1, 0)
        pg = h * dh
        part_x = px if part_x is None else part_x + px
        part_g = pg if part_g is None else part_g + pg
    high = part_g.astype(BF16)
    low = (part_g - high.astype(F32)).astype(BF16)
    ones = jnp.ones((SUBLANES, part_g.shape[1]), BF16)
    for target, places in zip(back, layout):
        for i, m in enumerate(places):
            rows = slice(m * capacity, (m + 1) * capacity)
            sums = contract(ones, high[rows, :], 1, 1) + contract(ones, low[rows, :], 1, 1)
            pack(target, i, capacity, part_x[rows, :], sums)


def weight_kernel(counts, capacity, quarter, *refs):
    n_msgs = sum(counts)
    msgs, refs = refs[:n_msgs], refs[n_msgs:]
    das, refs = refs[: len(counts)], refs[len(counts) :]
    dbs, refs = refs[: len(counts)], refs[len(counts) :]
    hs, outs = refs[: len(counts)], refs[len(counts) :]
    hidden = outs[2].shape[0]
    cols = slice(quarter * hidden, (quarter + 1) * hidden)
    x = jnp.concatenate([m[0:capacity, :] for m in msgs], axis=0)
    gw = jnp.concatenate([m[capacity:, :] for m in msgs], axis=0)
    da = jnp.concatenate([r[:, cols] for r in das], axis=0)
    db = jnp.concatenate([r[:, cols] for r in dbs], axis=0)
    h = jnp.concatenate([r[:, cols] for r in hs], axis=0)
    for out, total in zip(outs, (contract(x, da, 0, 0), contract(x, db, 0, 0), contract(h, gw, 0, 0))):
        out[...] = total.astype(out.dtype)


def add_kernel(*refs):
    for own, received, out in zip(refs[:3], refs[3:6], refs[6:]):
        out[...] = (own[...] + received[...].astype(F32)).astype(BF16)


def sum_kernel(n_parts, *refs):
    outs = refs[n_parts:]
    total = refs[0][...].astype(F32)
    for part in refs[1:n_parts]:
        total = total + part[...].astype(F32)
    rows = total.shape[0] // len(outs)
    for i, out in enumerate(outs):
        out[...] = total[i * rows : (i + 1) * rows, :].astype(BF16)


def unpack(messages, part, width, capacity):
    blocks = width // LANES
    base = part * (blocks * capacity + SUBLANES)
    values, sums = [], []
    for m in messages:
        cuts = [m[base + j * capacity : base + (j + 1) * capacity, :] for j in range(blocks)]
        values.append(jnp.concatenate(cuts, axis=1))
        tail = base + blocks * capacity
        sums.append(m[tail : tail + SUBLANES, 0:capacity])
    return jnp.concatenate(values, axis=0), sums


def gate_sums(experts, me, first, sums, table, capacity):
    total = jnp.zeros(experts.shape, F32)
    for i, row in enumerate(sums):
        value = contract(row, table[i * capacity : (i + 1) * capacity, :], 1, 0)
        total = total + jnp.where(experts == (me ^ (first + i)), value[0 : experts.shape[0], :], 0.0)
    return total


def mix_kernel(n_peers, near, capacity, me_ref, exp_ref, table_ref, *refs):
    routes, refs = refs[:n_peers], refs[n_peers:]
    messages, (sum_ref, gate_ref), targets = refs[:near], refs[near : near + 2], refs[near + 2 :]
    rows, width = sum_ref.shape
    table = table_ref[0 : near * capacity, :]
    values, sums = unpack(messages, 0, width, capacity)
    sum_ref[...] = contract(table, values, 0, 0)
    gate_ref[...] = gate_sums(exp_ref[...], me_ref[0], 0, sums, table, capacity)
    count = max(near, SUBLANES)
    for p in range(n_peers):
        experts = routes[p][0:2, :]
        hits = slot_tables(experts, partner_ids(count, rows, me_ref[0]), capacity)[:near]
        table = jnp.concatenate([jnp.where(hit, 1.0, 0.0).astype(BF16) for hit in hits], axis=0)
        values, sums = unpack(messages, p + 1, width, capacity)
        targets[p][0:rows, :] = contract(table, values, 0, 0).astype(BF16)
        targets[p][rows:, :] = jnp.zeros((SUBLANES, width), BF16)
        targets[p][rows : rows + 2, 0:rows] = gate_sums(experts, me_ref[0], 0, sums, table, capacity).astype(BF16)


def combine_kernel(near, n_peers, capacity, me_ref, exp_ref, ratio_ref, table_ref, sum_ref, gate_ref, *refs):
    parts, messages, (dtok_ref, dgate_ref) = refs[:n_peers], refs[n_peers:-2], refs[-2:]
    rows, width = dtok_ref.shape
    table = table_ref[near * capacity :, :]
    values, sums = unpack(messages, 0, width, capacity)
    total = sum_ref[...] + contract(table, values, 0, 0)
    d_gates = gate_ref[...] + gate_sums(exp_ref[...], me_ref[0], near, sums, table, capacity)
    for part in parts:
        total = total + part[0:rows, :].astype(F32)
        d_gates = d_gates + part[rows : rows + 2, 0:rows].astype(F32)
    dtok_ref[...] = total.astype(BF16)
    dgate_ref[...] = (d_gates * ratio_ref[...]).astype(BF16)


def call(body, outs, n_in, smem=0, hbm=0, scratch=()):
    def spec(space):
        return pl.BlockSpec(memory_space=space)

    outs = [out if isinstance(out, jax.ShapeDtypeStruct) else jax.ShapeDtypeStruct(out, BF16) for out in outs]
    return pl.pallas_call(
        body,
        out_shape=outs,
        in_specs=[spec(pltpu.SMEM)] * smem
        + [spec(pltpu.HBM)] * hbm
        + [spec(pltpu.VMEM)] * (n_in - smem - hbm),
        out_specs=[spec(pltpu.VMEM)] * len(outs),
        scratch_shapes=list(scratch),
        compiler_params=pltpu.CompilerParams(vmem_limit_bytes=VMEM_LIMIT),
    )


def quarters_of(n_experts):
    size = n_experts // 4
    return [list(range(i * size, (i + 1) * size)) for i in range(4)]


def groups_of(n_experts):
    first, second, third, fourth = quarters_of(n_experts)
    return [[first], [second], [third]] + [[[k]] for k in fourth]


def local_tiled(tokens, cotangent, gates, experts, keep, gate_w, up_w, down_w):
    return local_steps(tokens, cotangent, gates, experts, keep, gate_w, up_w, down_w)


def local_steps(tokens, cotangent, gates, experts, keep, gate_w, up_w, down_w):
    n_experts = lax.axis_size("ep")
    n_groups = lax.axis_size("zr")
    tok_rows, width = tokens.shape
    hidden = gate_w.shape[2]
    capacity = 3 * tok_rows // n_experts
    me = lax.axis_index("ep").astype(jnp.int32).reshape(1)
    route = (experts.T, keep.T, gates.T)

    def exchange(value, axis, size, bit):
        return lax.ppermute(value, axis, [(i, i ^ bit) for i in range(size)])

    def run(body, outs, *args, **kinds):
        return call(body, outs, len(args), **kinds)(*args)

    held = [pltpu.with_memory_space_constraint(w[0], pltpu.HBM) for w in (gate_w, up_w, down_w)]
    swapped = [exchange(w[0], "zr", n_groups, 1) for w in (gate_w, up_w, down_w)]
    sems = pltpu.SemaphoreType.DMA
    turned = [w.shape[::-1] for w in held]
    scratch = [pltpu.VMEM(held[2].shape, BF16), sems((3,))]
    held = run(stage_kernel, [w.shape for w in held[:2]] + turned, *held, hbm=3, scratch=scratch)
    weights = [*held, *swapped[:2], *run(turn_kernel, turned, *swapped)]

    inputs = [pltpu.with_memory_space_constraint(v, pltpu.HBM) for v in (*route, tokens, cotangent)]
    outs = [(n_experts * capacity, tok_rows), jax.ShapeDtypeStruct(route[0].shape, jnp.int32)]
    outs += [jax.ShapeDtypeStruct(route[0].shape, F32), jax.ShapeDtypeStruct((SUBLANES, tok_rows), jnp.int32)]
    outs += [(2 * capacity, width)] * n_experts
    table, named, ratio, shared, *sends = run(
        functools.partial(send_kernel, n_experts, capacity),
        outs,
        me,
        *inputs,
        smem=1,
        hbm=len(inputs),
        scratch=[pltpu.VMEM(v.shape, v.dtype) for v in inputs] + [sems((len(inputs),))],
    )
    mine = [exchange(sends[k], "ep", n_experts, k) if k else sends[0] for k in range(n_experts)]
    peers = list(range(2, n_groups, 2))
    theirs = [[exchange(mine[k], "zr", n_groups, r) for r in peers] for k in range(n_experts)]

    n_parts = 1 + len(peers)
    near = n_experts // 2
    msg_rows = width // LANES * capacity + SUBLANES
    all_msgs, counts, das, dbs, hs, returned = [], [], [], [], [], {}
    for chunks in groups_of(n_experts):
        group = sum(chunks, [])
        n_own = len(group)
        msgs = [mine[k] for k in group] + [theirs[k][p] for p in range(len(peers)) for k in group]
        if group[0] < near:
            layout = [[i + p * n_own for p in range(n_parts)] for i in range(n_own)]
        else:
            layout = [[group.index(k) + p * n_own for k in chunk] for p in range(n_parts) for chunk in chunks]
        outs = [(len(places) * msg_rows, LANES) for places in layout]
        outs += [(len(msgs) * capacity, 2 * hidden)] * 3
        body = functools.partial(grad_kernel, len(msgs), layout, capacity)
        *back, da, db, h = run(body, outs, *msgs, *weights)
        all_msgs, counts = all_msgs + msgs, counts + [len(msgs)]
        das, dbs, hs = das + [da], dbs + [db], hs + [h]
        if group[0] < near:
            for k, value in zip(group, back):
                returned[k] = exchange(value, "ep", n_experts, k) if k else value
            continue
        for c, chunk in enumerate(chunks):
            parts = [back[c]]
            for p, r in enumerate(peers):
                parts.append(exchange(back[(p + 1) * len(chunks) + c], "zr", n_groups, r))
            body = functools.partial(sum_kernel, n_parts)
            summed = run(body, [(msg_rows, LANES)] * len(chunk), *parts)
            for k, value in zip(chunk, summed):
                returned[k] = exchange(value, "ep", n_experts, k)

    found = [exchange(shared, "zr", n_groups, r) for r in peers]
    outs = [jax.ShapeDtypeStruct((tok_rows, width), F32), jax.ShapeDtypeStruct(named.shape, F32)]
    outs += [(tok_rows + SUBLANES, width)] * len(peers)
    near_sum, near_gates, *targets = run(
        functools.partial(mix_kernel, len(peers), near, capacity),
        outs,
        me,
        named,
        table,
        *found,
        *[returned[k] for k in range(near)],
        smem=1,
    )
    received = [exchange(value, "zr", n_groups, r) for value, r in zip(targets, peers)]
    near_args = (named, ratio, table, near_sum, near_gates, *received)

    shapes = [(width, hidden), (width, hidden), (hidden, width)]
    w_args = all_msgs + das + dbs + hs
    partner = run(functools.partial(weight_kernel, counts, capacity, 1), shapes, *w_args)
    swapped = [exchange(w, "zr", n_groups, 1) for w in partner]
    own = run(
        functools.partial(weight_kernel, counts, capacity, 0),
        [jax.ShapeDtypeStruct(shape, F32) for shape in shapes],
        *w_args,
    )
    dwg, dwu, dwd = run(add_kernel, shapes, *own, *swapped)

    d_tokens, d_gates = run(
        functools.partial(combine_kernel, near, len(peers), capacity),
        [(tok_rows, width), named.shape],
        me,
        *near_args,
        *[returned[k] for k in range(near, n_experts)],
        smem=1,
    )
    return d_tokens, d_gates.T, dwg[None], dwu[None], dwd[None]


def route_tables(experts, keep, gates, n_experts, capacity):
    tok_rows = experts.shape[0]
    flat_exp = experts.reshape(-1)
    onehot = (flat_exp[:, None] == jnp.arange(n_experts, dtype=jnp.int32)[None, :]).astype(
        jnp.int32
    )
    before = jnp.cumsum(onehot, axis=0) - onehot
    position = jnp.sum(before * onehot, axis=1)
    dest = (flat_exp * capacity + position).reshape(tok_rows, 2)
    slot_ids = jnp.arange(n_experts * capacity, dtype=jnp.int32)
    matches = dest[None, :, :] == slot_ids[:, None, None]
    table = jnp.any(matches, axis=2).astype(jnp.bfloat16)
    weight = gates.astype(jnp.float32) * keep.astype(jnp.float32)
    slot_weight = jnp.sum(jnp.where(matches, weight[None, :, :], 0.0), axis=(1, 2))
    return (table, dest, slot_weight)


def expert_grads(slot_input_rows, slot_g, slot_w, wg, wu, wd):
    pre_a = jnp.dot(slot_input_rows, wg, preferred_element_type=jnp.float32)
    pre_b = jnp.dot(slot_input_rows, wu, preferred_element_type=jnp.float32)
    sig = 1.0 / (1.0 + jnp.exp(-pre_a))
    act = pre_a * sig
    hidden_activation = act * pre_b
    value_gradient = jnp.einsum("sd,hd->sh", slot_g, wd, preferred_element_type=jnp.float32)
    scale = slot_w.astype(jnp.float32)[:, None]
    dh = scale * value_gradient
    gate_branch_gradient = (dh * pre_b * sig * (1.0 + pre_a * (1.0 - sig))).astype(jnp.bfloat16)
    up_branch_gradient = (dh * act).astype(jnp.bfloat16)
    hidden_w = (scale * hidden_activation).astype(jnp.bfloat16)
    dwg = jnp.einsum(
        "sd,sh->dh", slot_input_rows, gate_branch_gradient, preferred_element_type=jnp.float32
    ).astype(jnp.bfloat16)
    dwu = jnp.einsum(
        "sd,sh->dh", slot_input_rows, up_branch_gradient, preferred_element_type=jnp.float32
    ).astype(jnp.bfloat16)
    dwd = jnp.einsum("sh,sd->hd", hidden_w, slot_g, preferred_element_type=jnp.float32).astype(
        jnp.bfloat16
    )
    part_x = jnp.einsum("sh,dh->sd", gate_branch_gradient, wg, preferred_element_type=jnp.float32)
    part_x = part_x + jnp.einsum(
        "sh,dh->sd", up_branch_gradient, wu, preferred_element_type=jnp.float32
    )
    partial_gate_rows = jnp.sum(hidden_activation * value_gradient, axis=1)
    return (dwg, dwu, dwd, part_x.astype(jnp.bfloat16), partial_gate_rows.astype(jnp.bfloat16))


def local_general(tokens, cotangent, gates, experts, keep, gate_w, up_w, down_w):
    n_experts = lax.axis_size("ep")
    n_groups = lax.axis_size("zr")
    tok_rows = tokens.shape[0]
    width = tokens.shape[1]
    capacity = max(2, 3 * tok_rows // n_experts)
    flat_width = capacity * width
    table, dest, slot_weight = route_tables(experts, keep, gates, n_experts, capacity)
    send_x = jnp.dot(table, tokens, preferred_element_type=jnp.float32).astype(jnp.bfloat16)
    send_g = jnp.dot(table, cotangent, preferred_element_type=jnp.float32).astype(jnp.bfloat16)
    send_x = send_x.reshape(1, n_experts, flat_width)
    send_g = send_g.reshape(1, n_experts, flat_width)
    send_w = slot_weight.astype(jnp.bfloat16).reshape(1, n_experts, capacity)
    moved = (
        lax.all_to_all(send_x, "ep", split_axis=1, concat_axis=1, tiled=True),
        lax.all_to_all(send_g, "ep", split_axis=1, concat_axis=1, tiled=True),
        lax.all_to_all(send_w, "ep", split_axis=1, concat_axis=1, tiled=True),
    )
    arrived = (
        lax.all_gather(moved[0], "zr", axis=0, tiled=True),
        lax.all_gather(moved[1], "zr", axis=0, tiled=True),
        lax.all_gather(moved[2], "zr", axis=0, tiled=True),
    )
    slot_input_rows = arrived[0].reshape(-1, width)
    slot_g = arrived[1].reshape(-1, width)
    slot_w = arrived[2].reshape(-1)
    dwg, dwu, dwd, part_x, partial_gate_rows = expert_grads(
        slot_input_rows, slot_g, slot_w, gate_w[0], up_w[0], down_w[0]
    )
    part_x = part_x.reshape(n_groups, n_experts, flat_width)
    partial_gate_rows = partial_gate_rows.reshape(n_groups, n_experts, capacity)
    summed = (
        lax.psum_scatter(
            part_x.astype(jnp.float32).astype(jnp.bfloat16), "zr", scatter_dimension=0, tiled=True
        ).astype(jnp.float32),
        lax.psum_scatter(
            partial_gate_rows.astype(jnp.float32).astype(jnp.bfloat16),
            "zr",
            scatter_dimension=0,
            tiled=True,
        ).astype(jnp.float32),
    )
    rounded = (summed[0].astype(jnp.bfloat16), summed[1].astype(jnp.bfloat16))
    returned = (
        lax.all_to_all(rounded[0], "ep", split_axis=1, concat_axis=1, tiled=True),
        lax.all_to_all(rounded[1], "ep", split_axis=1, concat_axis=1, tiled=True),
    )
    slot_dx = returned[0]
    slot_dg = returned[1]
    slot_dx = slot_dx.reshape(n_experts * capacity, width)
    slot_dg = slot_dg.reshape(n_experts * capacity)
    d_tokens = jnp.einsum("st,sd->td", table, slot_dx, preferred_element_type=jnp.float32).astype(
        jnp.bfloat16
    )
    d_gates = jnp.take(slot_dg, dest) * keep.astype(jnp.bfloat16)
    return (d_tokens, d_gates, dwg[None], dwu[None], dwd[None])


def paired(mesh):
    counts = (mesh.shape["ep"], mesh.shape["zr"])
    return all(c > 2 and c & (c - 1) == 0 for c in counts)


def tiled(mesh, tokens):
    n_experts, n_groups = mesh.shape["ep"], mesh.shape["zr"]
    capacity = 3 * (tokens.shape[0] // (n_experts * n_groups)) // n_experts
    rows, width = tokens.shape[0] // (n_experts * n_groups), tokens.shape[1]
    aligned = capacity % 16 == 0 and capacity <= LANES and rows % 16 == 0 and rows <= width and width % LANES == 0
    return paired(mesh) and aligned


def solution(mesh):
    placed = (
        P(("ep", "zr"), None),
        P(("ep", "zr"), None),
        P(("ep", "zr"), None),
        P(("ep", "zr"), None),
        P(("ep", "zr"), None),
        P("ep", None, "zr"),
        P("ep", None, "zr"),
        P("ep", "zr", None),
    )

    def sharded(local):
        return jax.shard_map(
            local,
            mesh=mesh,
            in_specs=placed,
            out_specs=(
                P(("ep", "zr"), None),
                P(("ep", "zr"), None),
                P("ep", None, "zr"),
                P("ep", None, "zr"),
                P("ep", "zr", None),
            ),
            check_vma=False,
        )

    def step(tokens, *rest):
        chosen = local_tiled if tiled(mesh, tokens) else local_general
        return sharded(chosen)(tokens, *rest)

    return step
```
